32 devices in a mesh: lon: 8 (over z, core), lat: 4 (over y, x).
Axes of the slice: x: 2, y: 2, z: 4, core: 2. Of those that a mesh axis runs over, the one named last changes fastest.
Arguments:
- height: float32 [1, 1152, 4096], P(None, 'lat', 'lon'), may hold values from -6 to 6
- response: float32 [640], replicated, may hold values from 0.25 to 4
Outputs:
- loading: float32 [1, 1152, 4096], P(None, 'lat', 'lon')
The draws below stay inside these ranges and needn't reach their ends.
All inputs are finite; a program needn't handle non-finite values.
Results may differ from the reference program's by a relative error of at most 0.00085.
Values sent between devices are 32-bit elements; how exact they have to be, the bound alone decides.
A program may use at most 64 MiB of HBM per device.

```python
import math
import jax
import jax.numpy as jnp
from jax import lax

NLAT = 1152
NLON = 4096
MODES = 640
FIELDS = 1


def block_scale(stream_key, shape, split, least, high):
    loudness = 1.0
    for dim, parts in split:
        draws = jax.random.uniform(jax.random.fold_in(jax.random.fold_in(stream_key, 6), dim), (parts,), jnp.float32, least / len(split), high / len(split))
        loudness = loudness * jnp.repeat(jnp.exp(draws), shape[dim] // parts).reshape((-1,) + (1,) * (len(shape) - 1 - dim))
    return loudness


def centred(key, extent, width, reach, split=(), held_as=jnp.bfloat16):
    array = jax.random.normal(key, extent, jnp.float32) * width
    if len(split) > 0:
        array = block_scale(key, extent, split, -0.22, 0.18) * array
    return jnp.clip(array, min=-reach, max=reach).astype(held_as)


def setup_inputs(seed: int = 0) -> dict:
    splits = jax.random.split(jax.random.key(seed), 3)
    return {
        "height": centred(splits[0], (FIELDS, NLAT, NLON), 1.0, 6.0, ((1, 4), (2, 8)), jnp.float32),
        "response": jnp.clip(jnp.exp(jax.random.uniform(splits[1], (MODES,), jnp.float32, math.log(0.25), math.log(4.0))), 0.25, 4.0),
    }


block_degrees = 64
rescale_every = 8
highest = lax.Precision.HIGHEST

def colatitude_parts(latitudes):
    colatitude = (latitudes.astype(jnp.float32) + 0.5) * (jnp.pi / NLAT)
    sines = jnp.sin(colatitude)
    return (jnp.cos(colatitude), sines, sines * (jnp.pi / NLAT))

def legendre_sweep(cosines, sines, orders, consume, initial):
    order_float = orders.astype(jnp.float32)
    log_start = 0.5 * (lax.lgamma(order_float + 1.5) - lax.lgamma(order_float + 1.0) - lax.lgamma(jnp.full_like(order_float, 1.5))) - 0.5 * jnp.log(4.0 * jnp.pi)
    log_scale = log_start[:, None] + order_float[:, None] * jnp.log(sines)[None, :]
    zero_field = jnp.zeros(log_scale.shape, jnp.float32)

    def one_block(block_index, carried):
        earlier, latest, log_scale, running = carried
        first_degree = (block_index * block_degrees).astype(jnp.int32)
        factor = jnp.exp(log_scale)
        layers = []
        for offset in range(block_degrees):
            degree = first_degree + offset
            started = degree > orders
            starting = degree == orders
            degree_float = degree.astype(jnp.float32)
            lower_float = degree_float - 1.0
            square_gap = jnp.where(started, degree_float * degree_float - order_float * order_float, 1.0)
            growth = jnp.sqrt(jnp.where(started, (4.0 * degree_float * degree_float - 1.0) / square_gap, 0.0))
            damping = jnp.sqrt(jnp.where(started, (lower_float * lower_float - order_float * order_float) / jnp.maximum(4.0 * lower_float * lower_float - 1.0, 1.0), 0.0))
            current = jnp.where(starting[:, None], 1.0, growth[:, None] * (cosines[None, :] * latest - damping[:, None] * earlier))
            layers.append(current * factor)
            earlier, latest = (latest, current)
            if (offset + 1) % rescale_every == 0:
                largest = jnp.maximum(jnp.maximum(jnp.abs(earlier), jnp.abs(latest)), 1.0)
                earlier = earlier / largest
                latest = latest / largest
                log_scale = log_scale + jnp.log(largest)
                factor = jnp.exp(log_scale)
        legendre = jnp.stack(layers)
        return (earlier, latest, log_scale, consume(running, legendre, first_degree))
    carried = (zero_field, zero_field, log_scale, initial)
    carried = lax.fori_loop(0, MODES // block_degrees, one_block, carried)
    return carried[3]

def analyse(spectrum, latitudes, orders):
    cosines, sines, weights = colatitude_parts(latitudes)
    weighted = spectrum * weights

    def consume(coefficients, legendre, first_degree):
        block_terms = jnp.einsum('lmj,mcfj->lmcf', legendre, weighted, precision=highest)
        return lax.dynamic_update_slice_in_dim(coefficients, block_terms, first_degree, 0)
    initial = jnp.zeros((MODES,) + spectrum.shape[:3], jnp.float32)
    return legendre_sweep(cosines, sines, orders, consume, initial)

def synthesise(scaled, latitudes, orders):
    cosines, sines = colatitude_parts(latitudes)[:2]

    def consume(running, legendre, first_degree):
        scaled_block = lax.dynamic_slice_in_dim(scaled, first_degree, block_degrees, 0)
        return running + jnp.einsum('lmj,lmcf->mcfj', legendre, scaled_block, precision=highest)
    initial = jnp.zeros(scaled.shape[1:] + (latitudes.shape[0],), jnp.float32)
    return legendre_sweep(cosines, sines, orders, consume, initial)

def reference(height, response):
    transform = jnp.fft.rfft(height, axis=2)[:, :, :MODES] * (2.0 * jnp.pi / NLON)
    spectral_parts = jnp.stack([jnp.real(transform), jnp.imag(transform)], axis=0)
    spectral_parts = jnp.transpose(spectral_parts, (3, 0, 1, 2)).astype(jnp.float32)
    all_rows = jnp.arange(NLAT, dtype=jnp.int32)
    groups = spectral_parts.reshape((MODES // block_degrees, block_degrees) + spectral_parts.shape[1:])

    def one_group(group_pair):
        block_index, group_spectrum = group_pair
        orders = block_index * block_degrees + jnp.arange(block_degrees, dtype=jnp.int32)
        coefficients = analyse(group_spectrum, all_rows, orders)
        scaled = coefficients * response[:, None, None, None]
        return synthesise(scaled, all_rows, orders)
    synthesis = lax.map(one_group, (jnp.arange(MODES // block_degrees, dtype=jnp.int32), groups))
    synthesis = synthesis.reshape((MODES,) + synthesis.shape[2:])
    complex_parts = jnp.transpose(synthesis[:, 0] + 1j * synthesis[:, 1], (1, 2, 0))
    padded = jnp.pad(complex_parts, ((0, 0), (0, 0), (0, NLON // 2 + 1 - MODES)))
    loading = jnp.fft.irfft(padded, n=NLON, axis=2) * NLON
    return loading.astype(jnp.float32)
```

```python
import functools
import math

import jax
import jax.numpy as jnp
import numpy as np
from jax import lax
from jax.experimental import pallas as pl
from jax.experimental.pallas import tpu as pltpu
from jax.sharding import PartitionSpec as P

STEPS = 16
LANES = 128
RESCALE = 2.0 ** -64
THRESHOLD = 2.0 ** 32
high = lax.Precision.HIGH


def mode_order(modes, devices):
    count = modes // devices
    order = np.zeros((devices, count), np.int64)
    device = np.arange(devices)
    for slot in range((count + 1) // 2):
        order[:, slot] = slot * devices + device
        if slot != count - 1 - slot:
            order[:, count - 1 - slot] = modes - 1 - order[:, slot]
    return order


def sweep_kernel(resets, table, log_start, cosines, weights, out_first, out_second,
                 earlier, latest, log_scale, current_weights, sums):
    blocks = table.shape[0]
    groups = table.shape[1] // 8
    earlier[...] = jnp.zeros_like(earlier)
    latest[...] = jnp.zeros_like(latest)
    log_scale[...] = log_start[0]
    current_weights[...] = weights[0]
    sums[...] = jnp.zeros_like(sums)
    out_first[...] = jnp.zeros_like(out_first)

    def one_block(block, carry):
        @pl.when(resets[block] > 0)
        def _():
            switching = table[block][:, 48:49] > 0.5
            earlier[...] = jnp.where(switching, 0.0, earlier[...])
            latest[...] = jnp.where(switching, 0.0, latest[...])
            log_scale[...] = jnp.where(switching, log_start[1], log_scale[...])
            for parity in range(2):
                for part in range(2):
                    index = (parity, part)
                    current_weights[index] = jnp.where(
                        switching, weights[(1,) + index], current_weights[index]
                    )
                    out_first[index] = jnp.where(switching, sums[index], out_first[index])
                    sums[index] = jnp.where(switching, 0.0, sums[index])

        x = cosines[...]
        for group in range(groups):
            rows = pl.ds(group * 8, 8)
            columns = table[block, rows, :]
            before = earlier[rows, :]
            last = latest[rows, :]
            scale = log_scale[rows, :]
            factor = jnp.exp(scale)
            totals = [[None, None], [None, None]]
            for step in range(STEPS):
                growth = columns[:, step:step + 1]
                ratio = columns[:, STEPS + step:STEPS + step + 1]
                answer = columns[:, 2 * STEPS + step:2 * STEPS + step + 1]
                current = growth * (x * last) - ratio * before
                if step == 0:
                    current = current + columns[:, 49:50]
                before, last = last, current
                legendre = current * factor
                parity = step % 2
                for part in range(2):
                    product = legendre * current_weights[parity, part, rows, :]
                    coefficient = jnp.sum(product, axis=1, keepdims=True) * answer
                    term = legendre * coefficient
                    total = totals[parity][part]
                    totals[parity][part] = term if total is None else total + term
            for parity in range(2):
                for part in range(2):
                    sums[parity, part, rows, :] += totals[parity][part]
            large = jnp.maximum(jnp.abs(before), jnp.abs(last)) > THRESHOLD
            shrink = jnp.where(large, RESCALE, 1.0)
            earlier[rows, :] = before * shrink
            latest[rows, :] = last * shrink
            log_scale[rows, :] = scale + jnp.where(large, 64.0 * math.log(2.0), 0.0)
        return carry

    lax.fori_loop(0, blocks, one_block, 0)
    out_second[...] = sums[...]


def sweep(columns, response, device, devices, modes, cells):
    parts, slots, rows = columns.shape
    half = rows // 2
    padded_half = -(-half // LANES) * LANES
    chains = (slots + 1) // 2
    padded_chains = -(-chains // 8) * 8
    blocks = modes // STEPS + 1
    total_steps = blocks * STEPS

    chain = np.where(np.arange(padded_chains) < chains, np.arange(padded_chains), 0)
    first = jnp.asarray(chain * devices, jnp.int32) + device
    second = modes - 1 - first
    switch = ((modes - first + STEPS - 1) // STEPS) * STEPS
    step = jnp.arange(total_steps, dtype=jnp.int32)[:, None]
    in_first = step < switch[None, :]
    degree = jnp.where(in_first, first + step, second + step - switch)
    order = jnp.where(in_first, first, second)
    degree_float = degree.astype(jnp.float32)
    order_float = order.astype(jnp.float32)
    lower = degree_float - 1.0
    started = degree > order
    gap = jnp.where(started, degree_float * degree_float - order_float * order_float, 1.0)
    growth = jnp.where(
        started, jnp.sqrt((4.0 * degree_float * degree_float - 1.0) / gap), 0.0
    )
    damping = jnp.sqrt(
        jnp.where(
            started,
            (lower * lower - order_float * order_float)
            / jnp.maximum(4.0 * lower * lower - 1.0, 1.0),
            0.0,
        )
    )
    padded_response = jnp.pad(response, (STEPS, total_steps + STEPS))
    from_device = lax.dynamic_slice_in_dim(
        padded_response, STEPS + device, modes + STEPS
    )
    from_device = jnp.pad(from_device, (0, total_steps + (padded_chains + 1) * devices))
    first_response = jnp.stack(
        [from_device[c * devices:c * devices + total_steps] for c in chain], axis=1
    )
    offset = modes - 1 - device - ((modes - device + STEPS - 1) // STEPS) * STEPS
    second_response = lax.dynamic_slice_in_dim(
        padded_response, STEPS + offset, total_steps
    )[:, None]
    answers = jnp.where(in_first, first_response, second_response)
    blocked = [
        part.reshape(blocks, STEPS, padded_chains)
        for part in (growth, growth * damping, answers)
    ]
    block_first = jnp.arange(blocks, dtype=jnp.int32)[:, None, None] * STEPS
    switching = block_first == switch[None, None, :]
    starting = jnp.logical_or(switching, block_first == 0)
    flags = [switching.astype(jnp.float32), starting.astype(jnp.float32)]
    table = jnp.concatenate(blocked + flags, axis=1).transpose(0, 2, 1)
    table = jnp.pad(table, ((0, 0), (0, 0), (0, LANES - table.shape[2])))
    resets = jnp.any(switching, axis=(1, 2)).astype(jnp.int32)

    colatitude = (np.arange(padded_half) + 0.5) * (math.pi / rows)
    colatitude = np.where(np.arange(padded_half) < half, colatitude, math.pi / 2)
    cosines = np.broadcast_to(np.cos(colatitude).astype(np.float32), (8, padded_half))
    log_sines = jnp.asarray(np.log(np.sin(colatitude)).astype(np.float32))
    log_norm = np.array([
        0.5 * (math.lgamma(m + 1.5) - math.lgamma(1.5) - math.lgamma(m + 1.0))
        - 0.5 * math.log(4.0 * math.pi)
        for m in range(modes)
    ])
    per_device = mode_order(modes, devices)
    chosen = per_device[:, chain]
    starts = np.stack([log_norm[chosen], log_norm[modes - 1 - chosen]], axis=1)
    starts = lax.dynamic_index_in_dim(
        jnp.asarray(starts.astype(np.float32)), device, 0, keepdims=False
    )
    orders = jnp.stack([first, second]).astype(jnp.float32)
    log_start = starts[:, :, None] + orders[:, :, None] * log_sines

    spacing = 2.0 * math.pi / cells
    area = np.sin(colatitude) * (math.pi / rows) * spacing
    area = jnp.asarray(area[:half].astype(np.float32))
    slot_orders = lax.dynamic_index_in_dim(
        jnp.asarray(per_device.astype(np.int32)), device, 0, keepdims=False
    )
    gain = jnp.where(slot_orders == 0, 1.0, 2.0)[None, :, None] * area
    north = columns[:, :, :half]
    south = columns[:, :, half:][:, :, ::-1]
    folded = jnp.stack([(north + south) * gain, (north - south) * gain])
    pad_chain = ((0, 0), (0, 0), (0, padded_chains - chains), (0, padded_half - half))
    weights = jnp.stack([
        jnp.pad(folded[:, :, :chains], pad_chain),
        jnp.pad(folded[:, :, ::-1][:, :, :chains], pad_chain),
    ])

    shape = (padded_chains, padded_half)
    sums_shape = (2, parts) + shape
    vmem = pl.BlockSpec(memory_space=pltpu.VMEM)
    first_sums, second_sums = pl.pallas_call(
        sweep_kernel,
        out_shape=[jax.ShapeDtypeStruct(sums_shape, jnp.float32)] * 2,
        in_specs=[pl.BlockSpec(memory_space=pltpu.SMEM)] + [vmem] * 4,
        out_specs=[vmem] * 2,
        scratch_shapes=[pltpu.VMEM(shape, jnp.float32)] * 3
        + [pltpu.VMEM(sums_shape, jnp.float32)] * 2,
        name="legendre_sweep",
    )(resets, table, log_start, jnp.asarray(cosines), weights)
    partners = slots - chains
    joined = jnp.concatenate(
        [first_sums[:, :, :chains, :half], second_sums[:, :, :partners, :half][:, :, ::-1]],
        axis=2,
    )
    north = joined[0] + joined[1]
    south = (joined[0] - joined[1])[:, :, ::-1]
    return jnp.concatenate([north, south], axis=2)


def shards(modes, height, response):
    fields, band_rows, lon_cells = height.shape
    lon_count = lax.axis_size("lon")
    lat_count = lax.axis_size("lat")
    lon_index = lax.axis_index("lon")
    lat_index = lax.axis_index("lat")
    devices = lon_count * lat_count
    slots = modes // devices
    cells = lon_count * lon_cells
    device = lon_index * lat_count + lat_index

    order = mode_order(modes, devices)
    local = np.arange(lon_cells)
    angles = (order[:, :, None] * local % cells) * (2.0 * math.pi / cells)
    cos_table = jnp.asarray(np.cos(angles).astype(np.float32))
    sin_table = jnp.asarray(np.sin(angles).astype(np.float32))
    turn = (jnp.asarray(order.astype(np.int32)) * (lon_index * lon_cells) % cells)
    turn = turn.astype(jnp.float32)[:, :, None] * (2.0 * math.pi / cells)
    cos_turn, sin_turn = jnp.cos(turn), jnp.sin(turn)
    table = jnp.stack(
        [
            cos_turn * cos_table - sin_turn * sin_table,
            -(sin_turn * cos_table + cos_turn * sin_table),
        ],
        axis=1,
    ).reshape(2 * modes, lon_cells)

    outputs = []
    for field in range(fields):
        partial = lax.dot_general(
            table, height[field], (((1,), (1,)), ((), ())), precision=high,
            preferred_element_type=jnp.float32,
        )
        spectrum = lax.psum_scatter(partial, "lon", scatter_dimension=0, tiled=True)
        columns = lax.all_to_all(spectrum, "lat", split_axis=0, concat_axis=1, tiled=True)
        columns = columns.reshape(2, slots, lat_count * band_rows)
        synthesis = sweep(columns, response, device, devices, modes, cells)
        synthesis = synthesis.reshape(2 * slots, lat_count * band_rows)
        bands = lax.all_to_all(synthesis, "lat", split_axis=1, concat_axis=0, tiled=True)
        gathered = lax.all_gather(bands, "lon", axis=0, tiled=True)
        outputs.append(lax.dot_general(
            gathered, table, (((0,), (0,)), ((), ())), precision=high,
            preferred_element_type=jnp.float32,
        ))
    return jnp.stack(outputs)


def solution(mesh):
    placed = (P(None, "lat", "lon"), P())

    def loading(height, response):
        body = functools.partial(shards, response.shape[0])
        return jax.shard_map(
            body, mesh=mesh, in_specs=placed, out_specs=P(None, "lat", "lon"), check_vma=False
        )(height, response)

    return loading
```

```python
import functools
import math

import jax
import jax.numpy as jnp
import numpy as np
from jax import lax
from jax.experimental import pallas as pl
from jax.experimental.pallas import tpu as pltpu
from jax.sharding import PartitionSpec as P

STEPS = 16
LANES = 128
RESCALE = 2.0 ** -64
THRESHOLD = 2.0 ** 32
high = lax.Precision.HIGH


def mode_order(modes, devices):
    count = modes // devices
    order = np.zeros((devices, count), np.int64)
    device = np.arange(devices)
    for slot in range((count + 1) // 2):
        order[:, slot] = slot * devices + device
        if slot != count - 1 - slot:
            order[:, count - 1 - slot] = modes - 1 - order[:, slot]
    return order


exact = lax.Precision.HIGHEST


def dot(left, right):
    return jnp.dot(left, right, precision=exact, preferred_element_type=jnp.float32)


def sweep_kernel(modes, devices, slots, where, answers, second_answers, log_start, grid,
                 gains, columns, out, earlier, latest, log_scale, weights, current_weights,
                 first_sums, sums, ladder, partial, mirror):
    blocks = second_answers.shape[0]
    padded_chains, padded_half = latest.shape
    chains = (slots + 1) // 2
    groups = padded_chains // 8
    half = columns.shape[1] // 2
    south_start = columns.shape[1] - padded_half
    device = where[0]

    shape = (4 * padded_chains, columns.shape[0])
    row = lax.broadcasted_iota(jnp.int32, shape, 0)
    column = lax.broadcasted_iota(jnp.int32, shape, 1)
    chain = row % padded_chains
    part = (row // padded_chains) % 2
    second_side = row // (2 * padded_chains)
    slot = jnp.where(second_side == 1, slots - 1 - chain, chain)
    valid = jnp.logical_and(chain < chains, jnp.logical_or(second_side == 0, slot >= chains))
    select = jnp.where(
        jnp.logical_and(valid, column == part * slots + slot), 1.0, 0.0
    ).astype(jnp.float32)
    square = (padded_half, padded_half)
    mirror[...] = jnp.where(
        lax.broadcasted_iota(jnp.int32, square, 0) + lax.broadcasted_iota(jnp.int32, square, 1)
        == padded_half - 1, 1.0, 0.0,
    ).astype(jnp.float32)
    gain = gains[...] * grid[1:2, :]
    north = dot(select, columns[:, :padded_half])
    south = dot(dot(select, columns[:, south_start:]), mirror[...])
    weights[0] = (north + south) * gain
    weights[1] = (north - south) * gain

    earlier[...] = jnp.zeros_like(earlier)
    latest[...] = jnp.zeros_like(latest)
    log_scale[...] = log_start[0]
    current_weights[...] = weights[:, :2 * padded_chains, :]
    sums[...] = jnp.zeros_like(sums)
    first_sums[...] = jnp.zeros_like(first_sums)
    ones = jnp.ones((2 * LANES, LANES), jnp.bfloat16)
    top_switch = (modes - device + STEPS - 1) // STEPS
    stride = devices // STEPS

    def one_block(block, carry):
        behind = top_switch - block
        any_reset = jnp.logical_and(
            behind >= 0, jnp.logical_and(behind % stride == 0, behind < padded_chains * stride)
        )

        @pl.when(any_reset)
        def _():
            shape = (padded_chains, padded_half)
            chain = lax.broadcasted_iota(jnp.int32, shape, 0)
            switching = jnp.where(chain < chains, chain, 0) * stride == behind
            earlier[...] = jnp.where(switching, 0.0, earlier[...])
            latest[...] = jnp.where(switching, 0.0, latest[...])
            log_scale[...] = jnp.where(switching, log_start[1], log_scale[...])
            for parity in range(2):
                for part in range(2):
                    rows = pl.ds(part * padded_chains, padded_chains)
                    later = pl.ds((2 + part) * padded_chains, padded_chains)
                    current_weights[parity, rows, :] = jnp.where(
                        switching, weights[parity, later, :], current_weights[parity, rows, :]
                    )
                    held = sums[parity, rows, :]
                    first_sums[parity, rows, :] = jnp.where(
                        switching, held, first_sums[parity, rows, :]
                    )
                    sums[parity, rows, :] = jnp.where(switching, 0.0, held)

        x = grid[0:1, :]
        reduced = []
        for group in range(groups):
            rows = pl.ds(group * 8, 8)
            tile = (8, LANES)
            chain = lax.broadcasted_iota(jnp.int32, tile, 0) + group * 8
            chain = jnp.where(chain < chains, chain, 0)
            lane = lax.broadcasted_iota(jnp.int32, tile, 1)
            first = chain * devices + device
            switch = top_switch - chain * stride
            is_first = block < switch
            order = jnp.where(is_first, first, modes - 1 - first)
            step = jnp.where(is_first, block, block - switch) * STEPS + lane
            started = step > 0
            n = order.astype(jnp.float32)
            k = jnp.maximum(step, 1).astype(jnp.float32)
            degree = n + k
            lower = degree - 1.0
            growths = jnp.where(started, jnp.sqrt(
                (4.0 * degree * degree - 1.0) / (k * (degree + n))), 0.0)
            ratios = growths * jnp.sqrt(jnp.where(
                started, (k - 1.0) * (lower + n) / jnp.maximum(4.0 * lower * lower - 1.0, 1.0), 0.0))
            starts = jnp.where(step == 0, 1.0, 0.0)[:, 0:1]
            replies = jnp.where(
                is_first,
                answers[pl.ds(block + group * 8 * stride, 8, stride=stride), :],
                jnp.broadcast_to(second_answers[pl.ds(block, 1), :], tile),
            )
            before = earlier[rows, :]
            last = latest[rows, :]
            scale = log_scale[rows, :]
            factor = jnp.exp(scale)
            for step in range(STEPS):
                current = growths[:, step:step + 1] * (x * last) - ratios[:, step:step + 1] * before
                if step == 0:
                    current = current + starts
                before, last = last, current
                legendre = current * factor
                ladder[group, step] = legendre
                reply = replies[:, step:step + 1]
                for part in range(2):
                    held = current_weights[step % 2, pl.ds(part * padded_chains + group * 8, 8), :]
                    total = None
                    for lanes in range(0, padded_half, LANES):
                        term = legendre[:, lanes:lanes + LANES] * held[:, lanes:lanes + LANES]
                        total = term if total is None else total + term
                    partial[group, pl.ds((part * STEPS + step) * 8, 8), :] = total * reply
            large = jnp.maximum(jnp.abs(before), jnp.abs(last)) > THRESHOLD
            shrink = jnp.where(large, RESCALE, 1.0)
            earlier[rows, :] = before * shrink
            latest[rows, :] = last * shrink
            log_scale[rows, :] = scale + jnp.where(large, 64.0 * math.log(2.0), 0.0)
            value = partial[group]
            upper = value.astype(jnp.bfloat16)
            rest = (value - upper.astype(jnp.float32)).astype(jnp.bfloat16)
            reduced.append(jnp.dot(
                jnp.concatenate([upper, rest], axis=1), ones,
                preferred_element_type=jnp.float32,
            ))
        for group in range(groups):
            partial[group] = reduced[group]
        for group in range(groups):
            for lanes in range(0, padded_half, LANES):
                totals = [[None, None], [None, None]]
                for step in range(STEPS):
                    legendre = ladder[group, step, :, pl.ds(lanes, LANES)]
                    for part in range(2):
                        term = legendre * partial[group, pl.ds((part * STEPS + step) * 8, 8), :]
                        total = totals[step % 2][part]
                        totals[step % 2][part] = term if total is None else total + term
                for parity in range(2):
                    for part in range(2):
                        rows = pl.ds(part * padded_chains + group * 8, 8)
                        sums[parity, rows, pl.ds(lanes, LANES)] += totals[parity][part]
        return carry

    lax.fori_loop(0, blocks, one_block, 0)
    both = [jnp.concatenate([first_sums[p], sums[p]], axis=0) for p in range(2)]
    shape = (columns.shape[0], 4 * padded_chains)
    row = lax.broadcasted_iota(jnp.int32, shape, 0)
    column = lax.broadcasted_iota(jnp.int32, shape, 1)
    part, slot = row // slots, row % slots
    side = jnp.where(slot < chains, 0, 1)
    chain = jnp.where(slot < chains, slot, slots - 1 - slot)
    back = jnp.where(
        column == (side * 2 + part) * padded_chains + chain, 1.0, 0.0
    ).astype(jnp.float32)
    north = dot(back, both[0] + both[1])
    south = dot(dot(back, both[0] - both[1]), mirror[...])
    out[:, :south_start] = north[:, :south_start]
    overlap = padded_half - south_start
    lane = lax.broadcasted_iota(jnp.int32, (columns.shape[0], overlap), 1) + south_start
    out[:, south_start:padded_half] = jnp.where(
        lane < half, north[:, south_start:], south[:, :overlap]
    )
    out[:, padded_half:] = south[:, overlap:]


def sweep(columns, response, device, devices, modes, cells):
    rows = columns.shape[1]
    slots = columns.shape[0] // 2
    half = rows // 2
    padded_half = -(-half // LANES) * LANES
    chains = (slots + 1) // 2
    padded_chains = -(-chains // 8) * 8
    blocks = modes // STEPS + 1
    total_steps = blocks * STEPS

    lanes = ((0, 0), (0, LANES - STEPS))
    count = blocks + padded_chains * devices // STEPS
    padded_response = jnp.pad(response, (STEPS, (count + 2) * STEPS + devices))
    answers = lax.dynamic_slice_in_dim(padded_response, STEPS + device, count * STEPS)
    offset = modes - 1 - device - ((modes - device + STEPS - 1) // STEPS) * STEPS
    second_answers = lax.dynamic_slice_in_dim(padded_response, STEPS + offset, total_steps)
    answers = jnp.pad(answers.reshape(count, STEPS), lanes)
    second_answers = jnp.pad(second_answers.reshape(blocks, STEPS), lanes)

    inside = np.arange(padded_half) < half
    colatitude = (np.arange(padded_half) + 0.5) * (math.pi / rows)
    colatitude = np.where(inside, colatitude, math.pi / 2)
    area = np.sin(colatitude) * (math.pi / rows) * (2.0 * math.pi / cells)
    grid = np.zeros((8, padded_half), np.float32)
    grid[0] = np.cos(colatitude)
    grid[1] = np.where(inside, area, 0.0)
    log_sines = jnp.asarray(np.log(np.sin(colatitude)).astype(np.float32))
    log_norm = np.array([
        0.5 * (math.lgamma(m + 1.5) - math.lgamma(1.5) - math.lgamma(m + 1.0))
        - 0.5 * math.log(4.0 * math.pi)
        for m in range(modes)
    ])
    chain = np.where(np.arange(padded_chains) < chains, np.arange(padded_chains), 0)
    first = np.arange(devices)[:, None] + chain * devices
    orders = np.stack([first, modes - 1 - first], axis=1)
    packed = np.stack([log_norm[orders], orders, np.where(orders == 0, 1.0, 2.0)], axis=1)
    packed = lax.dynamic_index_in_dim(
        jnp.asarray(packed.astype(np.float32)), device, 0, keepdims=False
    )
    log_start = packed[0][:, :, None] + packed[1][:, :, None] * log_sines
    gains = jnp.broadcast_to(packed[2][:, None, :], (2, 2, padded_chains))
    gains = gains.reshape(4 * padded_chains, 1)

    vmem = pl.BlockSpec(memory_space=pltpu.VMEM)
    state = pltpu.VMEM((padded_chains, padded_half), jnp.float32)
    pair = pltpu.VMEM((2, 2 * padded_chains, padded_half), jnp.float32)
    groups = padded_chains // 8
    return pl.pallas_call(
        functools.partial(sweep_kernel, modes, devices, slots),
        out_shape=jax.ShapeDtypeStruct(columns.shape, jnp.float32),
        in_specs=[pl.BlockSpec(memory_space=pltpu.SMEM)] + [vmem] * 6,
        out_specs=vmem,
        scratch_shapes=[
            state, state, state,
            pltpu.VMEM((2, 4 * padded_chains, padded_half), jnp.float32),
            pair, pair, pair,
            pltpu.VMEM((groups, STEPS, 8, padded_half), jnp.float32),
            pltpu.VMEM((groups, 2 * STEPS * 8, LANES), jnp.float32),
            pltpu.VMEM((padded_half, padded_half), jnp.float32),
        ],
        name="legendre_sweep",
    )(device.reshape(1), answers, second_answers, log_start, jnp.asarray(grid), gains, columns)


def shards(modes, height, response):
    fields, band_rows, lon_cells = height.shape
    lon_count = lax.axis_size("lon")
    lat_count = lax.axis_size("lat")
    lon_index = lax.axis_index("lon")
    lat_index = lax.axis_index("lat")
    devices = lon_count * lat_count
    cells = lon_count * lon_cells
    device = lon_index * lat_count + lat_index

    order = mode_order(modes, devices)
    local = np.arange(lon_cells)
    angles = (order[:, :, None] * local % cells) * (2.0 * math.pi / cells)
    cos_table = jnp.asarray(np.cos(angles).astype(np.float32))
    sin_table = jnp.asarray(np.sin(angles).astype(np.float32))
    turn = (jnp.asarray(order.astype(np.int32)) * (lon_index * lon_cells) % cells)
    turn = turn.astype(jnp.float32)[:, :, None] * (2.0 * math.pi / cells)
    cos_turn, sin_turn = jnp.cos(turn), jnp.sin(turn)
    table = jnp.stack(
        [
            cos_turn * cos_table - sin_turn * sin_table,
            -(sin_turn * cos_table + cos_turn * sin_table),
        ],
        axis=1,
    ).reshape(2 * modes, lon_cells)

    outputs = []
    for field in range(fields):
        partial = lax.dot_general(
            table, height[field], (((1,), (1,)), ((), ())), precision=high,
            preferred_element_type=jnp.float32,
        )
        spectrum = lax.psum_scatter(partial, "lon", scatter_dimension=0, tiled=True)
        columns = lax.all_to_all(spectrum, "lat", split_axis=0, concat_axis=1, tiled=True)
        synthesis = sweep(columns, response, device, devices, modes, cells)
        bands = lax.all_to_all(synthesis, "lat", split_axis=1, concat_axis=0, tiled=True)
        gathered = lax.all_gather(bands, "lon", axis=0, tiled=True)
        outputs.append(lax.dot_general(
            gathered, table, (((0,), (0,)), ((), ())), precision=high,
            preferred_element_type=jnp.float32,
        ))
    return jnp.stack(outputs)


def solution(mesh):
    placed = (P(None, "lat", "lon"), P())

    def loading(height, response):
        body = functools.partial(shards, response.shape[0])
        return jax.shard_map(
            body, mesh=mesh, in_specs=placed, out_specs=P(None, "lat", "lon"), check_vma=False
        )(height, response)

    return loading
```

```python
import functools
import math

import jax
import jax.numpy as jnp
import numpy as np
from jax import lax
from jax.experimental import pallas as pl
from jax.experimental.pallas import tpu as pltpu
from jax.sharding import PartitionSpec as P

STEPS = 16
LANES = 128
RESCALE = 2.0 ** -64
THRESHOLD = 2.0 ** 32
high = lax.Precision.HIGH


def mode_order(modes, devices):
    count = modes // devices
    order = np.zeros((devices, count), np.int64)
    device = np.arange(devices)
    for slot in range((count + 1) // 2):
        order[:, slot] = slot * devices + device
        if slot != count - 1 - slot:
            order[:, count - 1 - slot] = modes - 1 - order[:, slot]
    return order


exact = lax.Precision.HIGHEST


def dot(left, right):
    return jnp.dot(left, right, precision=exact, preferred_element_type=jnp.float32)


def sweep_kernel(modes, devices, slots, where, answers, second_answers, log_start, grid,
                 gains, columns, out, earlier, latest, log_scale, weights, current_weights,
                 first_sums, sums, ladder, partial, mirror):
    blocks = second_answers.shape[0]
    padded_chains, padded_half = latest.shape
    chains = (slots + 1) // 2
    groups = padded_chains // 8
    half = columns.shape[1] // 2
    south_start = columns.shape[1] - padded_half
    device = where[0]

    shape = (4 * padded_chains, columns.shape[0])
    row = lax.broadcasted_iota(jnp.int32, shape, 0)
    column = lax.broadcasted_iota(jnp.int32, shape, 1)
    chain = row % padded_chains
    part = (row // padded_chains) % 2
    second_side = row // (2 * padded_chains)
    slot = jnp.where(second_side == 1, slots - 1 - chain, chain)
    valid = jnp.logical_and(chain < chains, jnp.logical_or(second_side == 0, slot >= chains))
    select = jnp.where(
        jnp.logical_and(valid, column == part * slots + slot), 1.0, 0.0
    ).astype(jnp.float32)
    square = (padded_half, padded_half)
    mirror[...] = jnp.where(
        lax.broadcasted_iota(jnp.int32, square, 0) + lax.broadcasted_iota(jnp.int32, square, 1)
        == padded_half - 1, 1.0, 0.0,
    ).astype(jnp.float32)
    gain = gains[...] * grid[1:2, :]
    north = dot(select, columns[:, :padded_half])
    south = dot(dot(select, columns[:, south_start:]), mirror[...])
    weights[0] = (north + south) * gain
    weights[1] = (north - south) * gain

    earlier[...] = jnp.zeros_like(earlier)
    latest[...] = jnp.zeros_like(latest)
    log_scale[...] = log_start[0]
    current_weights[...] = weights[:, :2 * padded_chains, :]
    sums[...] = jnp.zeros_like(sums)
    first_sums[...] = jnp.zeros_like(first_sums)
    ones = jnp.ones((2 * LANES, LANES), jnp.bfloat16)
    top_switch = (modes - device + STEPS - 1) // STEPS
    stride = devices // STEPS

    def one_block(block, carry):
        behind = top_switch - block
        any_reset = jnp.logical_and(
            behind >= 0, jnp.logical_and(behind % stride == 0, behind < padded_chains * stride)
        )

        @pl.when(any_reset)
        def _():
            shape = (padded_chains, padded_half)
            chain = lax.broadcasted_iota(jnp.int32, shape, 0)
            switching = jnp.where(chain < chains, chain, 0) * stride == behind
            earlier[...] = jnp.where(switching, 0.0, earlier[...])
            latest[...] = jnp.where(switching, 0.0, latest[...])
            log_scale[...] = jnp.where(switching, log_start[1], log_scale[...])
            for parity in range(2):
                for part in range(2):
                    rows = pl.ds(part * padded_chains, padded_chains)
                    later = pl.ds((2 + part) * padded_chains, padded_chains)
                    current_weights[parity, rows, :] = jnp.where(
                        switching, weights[parity, later, :], current_weights[parity, rows, :]
                    )
                    held = sums[parity, rows, :]
                    first_sums[parity, rows, :] = jnp.where(
                        switching, held, first_sums[parity, rows, :]
                    )
                    sums[parity, rows, :] = jnp.where(switching, 0.0, held)

        x = grid[0:1, :]
        reduced = []
        for group in range(groups):
            rows = pl.ds(group * 8, 8)
            tile = (8, LANES)
            chain = lax.broadcasted_iota(jnp.int32, tile, 0) + group * 8
            chain = jnp.where(chain < chains, chain, 0)
            lane = lax.broadcasted_iota(jnp.int32, tile, 1)
            first = chain * devices + device
            switch = top_switch - chain * stride
            is_first = block < switch
            order = jnp.where(is_first, first, modes - 1 - first)
            step = jnp.where(is_first, block, block - switch) * STEPS + lane
            started = step > 0
            n = order.astype(jnp.float32)
            k = jnp.maximum(step, 1).astype(jnp.float32)
            degree = n + k
            lower = degree - 1.0
            growths = jnp.where(started, jnp.sqrt(
                (4.0 * degree * degree - 1.0) / (k * (degree + n))), 0.0)
            ratios = growths * jnp.sqrt(jnp.where(
                started, (k - 1.0) * (lower + n) / jnp.maximum(4.0 * lower * lower - 1.0, 1.0), 0.0))
            starts = jnp.where(step == 0, 1.0, 0.0)[:, 0:1]
            replies = jnp.where(
                is_first,
                answers[pl.ds(block + group * 8 * stride, 8, stride=stride), :],
                jnp.broadcast_to(second_answers[pl.ds(block, 1), :], tile),
            )
            before = earlier[rows, :]
            last = latest[rows, :]
            scale = log_scale[rows, :]
            factor = jnp.exp(scale)
            for step in range(STEPS):
                current = growths[:, step:step + 1] * (x * last) - ratios[:, step:step + 1] * before
                if step == 0:
                    current = current + starts
                before, last = last, current
                legendre = current * factor
                ladder[group, step] = legendre
                reply = replies[:, step:step + 1]
                for part in range(2):
                    held = current_weights[step % 2, pl.ds(part * padded_chains + group * 8, 8), :]
                    total = None
                    for lanes in range(0, padded_half, LANES):
                        term = legendre[:, lanes:lanes + LANES] * held[:, lanes:lanes + LANES]
                        total = term if total is None else total + term
                    partial[group, pl.ds((part * STEPS + step) * 8, 8), :] = total * reply
            large = jnp.maximum(jnp.abs(before), jnp.abs(last)) > THRESHOLD
            shrink = jnp.where(large, RESCALE, 1.0)
            earlier[rows, :] = before * shrink
            latest[rows, :] = last * shrink
            log_scale[rows, :] = scale + jnp.where(large, 64.0 * math.log(2.0), 0.0)
            value = partial[group]
            upper = value.astype(jnp.bfloat16)
            rest = (value - upper.astype(jnp.float32)).astype(jnp.bfloat16)
            reduced.append(jnp.dot(
                jnp.concatenate([upper, rest], axis=1), ones,
                preferred_element_type=jnp.float32,
            ))
        for group in range(groups):
            partial[group] = reduced[group]
        for group in range(groups):
            for lanes in range(0, padded_half, LANES):
                totals = [[None, None], [None, None]]
                for step in range(STEPS):
                    legendre = ladder[group, step, :, pl.ds(lanes, LANES)]
                    for part in range(2):
                        term = legendre * partial[group, pl.ds((part * STEPS + step) * 8, 8), :]
                        total = totals[step % 2][part]
                        totals[step % 2][part] = term if total is None else total + term
                for parity in range(2):
                    for part in range(2):
                        rows = pl.ds(part * padded_chains + group * 8, 8)
                        sums[parity, rows, pl.ds(lanes, LANES)] += totals[parity][part]
        return carry

    lax.fori_loop(0, blocks, one_block, 0)
    both = [jnp.concatenate([first_sums[p], sums[p]], axis=0) for p in range(2)]
    shape = (columns.shape[0], 4 * padded_chains)
    row = lax.broadcasted_iota(jnp.int32, shape, 0)
    column = lax.broadcasted_iota(jnp.int32, shape, 1)
    part, slot = row // slots, row % slots
    side = jnp.where(slot < chains, 0, 1)
    chain = jnp.where(slot < chains, slot, slots - 1 - slot)
    back = jnp.where(
        column == (side * 2 + part) * padded_chains + chain, 1.0, 0.0
    ).astype(jnp.float32)
    north = dot(back, both[0] + both[1])
    south = dot(dot(back, both[0] - both[1]), mirror[...])
    out[:, :south_start] = north[:, :south_start]
    overlap = padded_half - south_start
    lane = lax.broadcasted_iota(jnp.int32, (columns.shape[0], overlap), 1) + south_start
    out[:, south_start:padded_half] = jnp.where(
        lane < half, north[:, south_start:], south[:, :overlap]
    )
    out[:, padded_half:] = south[:, overlap:]


def sweep(columns, response, device, devices, modes, cells):
    rows = columns.shape[1]
    slots = columns.shape[0] // 2
    half = rows // 2
    padded_half = -(-half // LANES) * LANES
    chains = (slots + 1) // 2
    padded_chains = -(-chains // 8) * 8
    blocks = modes // STEPS + 1
    total_steps = blocks * STEPS

    lanes = ((0, 0), (0, LANES - STEPS))
    count = blocks + padded_chains * devices // STEPS
    padded_response = jnp.pad(response, (STEPS, (count + 2) * STEPS + devices))
    answers = lax.dynamic_slice_in_dim(padded_response, STEPS + device, count * STEPS)
    offset = modes - 1 - device - ((modes - device + STEPS - 1) // STEPS) * STEPS
    second_answers = lax.dynamic_slice_in_dim(padded_response, STEPS + offset, total_steps)
    answers = jnp.pad(answers.reshape(count, STEPS), lanes)
    second_answers = jnp.pad(second_answers.reshape(blocks, STEPS), lanes)

    inside = np.arange(padded_half) < half
    colatitude = (np.arange(padded_half) + 0.5) * (math.pi / rows)
    colatitude = np.where(inside, colatitude, math.pi / 2)
    area = np.sin(colatitude) * (math.pi / rows) * (2.0 * math.pi / cells)
    grid = np.zeros((8, padded_half), np.float32)
    grid[0] = np.cos(colatitude)
    grid[1] = np.where(inside, area, 0.0)
    log_sines = jnp.asarray(np.log(np.sin(colatitude)).astype(np.float32))
    log_norm = np.array([
        0.5 * (math.lgamma(m + 1.5) - math.lgamma(1.5) - math.lgamma(m + 1.0))
        - 0.5 * math.log(4.0 * math.pi)
        for m in range(modes)
    ])
    chain = np.where(np.arange(padded_chains) < chains, np.arange(padded_chains), 0)
    first = np.arange(devices)[:, None] + chain * devices
    orders = np.stack([first, modes - 1 - first], axis=1)
    packed = np.stack([log_norm[orders], orders, np.where(orders == 0, 1.0, 2.0)], axis=1)
    packed = lax.dynamic_index_in_dim(
        jnp.asarray(packed.astype(np.float32)), device, 0, keepdims=False
    )
    log_start = packed[0][:, :, None] + packed[1][:, :, None] * log_sines
    gains = jnp.broadcast_to(packed[2][:, None, :], (2, 2, padded_chains))
    gains = gains.reshape(4 * padded_chains, 1)

    vmem = pl.BlockSpec(memory_space=pltpu.VMEM)
    state = pltpu.VMEM((padded_chains, padded_half), jnp.float32)
    pair = pltpu.VMEM((2, 2 * padded_chains, padded_half), jnp.float32)
    groups = padded_chains // 8
    return pl.pallas_call(
        functools.partial(sweep_kernel, modes, devices, slots),
        out_shape=jax.ShapeDtypeStruct(columns.shape, jnp.float32),
        in_specs=[pl.BlockSpec(memory_space=pltpu.SMEM)] + [vmem] * 6,
        out_specs=vmem,
        scratch_shapes=[
            state, state, state,
            pltpu.VMEM((2, 4 * padded_chains, padded_half), jnp.float32),
            pair, pair, pair,
            pltpu.VMEM((groups, STEPS, 8, padded_half), jnp.float32),
            pltpu.VMEM((groups, 2 * STEPS * 8, LANES), jnp.float32),
            pltpu.VMEM((padded_half, padded_half), jnp.float32),
        ],
        name="legendre_sweep",
    )(device.reshape(1), answers, second_answers, log_start, jnp.asarray(grid), gains, columns)


def gather_kernel(count, block_ref, out_ref, send, receive):
    me = lax.axis_index("lon")
    core, chip, chips = me % 2, me // 2, count // 2
    partner = chip * 2 + 1 - core
    rows = block_ref.shape[0]
    peers = [((chip + k) % chips) * 2 + core for k in range(1, chips)]
    barrier = pltpu.get_barrier_semaphore()
    for peer in peers + [partner]:
        pl.semaphore_signal(
            barrier, inc=1, device_id={"lon": peer}, device_id_type=pl.DeviceIdType.MESH
        )
    pl.semaphore_wait(barrier, chips)

    def push(source, owner, target, index):
        copy = pltpu.make_async_remote_copy(
            src_ref=source,
            dst_ref=out_ref.at[pl.ds(pl.multiple_of(owner * rows, 8), rows)],
            send_sem=send.at[index],
            recv_sem=receive.at[index],
            device_id={"lon": target},
            device_id_type=pl.DeviceIdType.MESH,
        )
        copy.start()
        return copy

    copies = [push(block_ref, me, peer, k) for k, peer in enumerate(peers)]
    shared = [push(block_ref, me, partner, chips - 1)]
    out_ref[pl.ds(pl.multiple_of(me * rows, 8), rows), :] = block_ref[...]
    for k in list(range(0, chips - 1, 2)) + list(range(1, chips - 1, 2)):
        copies[k].wait_recv()
        owner = ((chip + chips - 1 - k) % chips) * 2 + core
        arrived = out_ref.at[pl.ds(pl.multiple_of(owner * rows, 8), rows)]
        shared.append(push(arrived, owner, partner, chips + k))
    for copy in copies:
        copy.wait_send()
    for copy in shared:
        copy.wait()


def gather(block, count):
    vmem = pl.BlockSpec(memory_space=pltpu.VMEM)
    copies = count - 1
    return pl.pallas_call(
        functools.partial(gather_kernel, count),
        out_shape=jax.ShapeDtypeStruct((count * block.shape[0], block.shape[1]), block.dtype),
        in_specs=[vmem],
        out_specs=vmem,
        scratch_shapes=[pltpu.SemaphoreType.DMA((copies,)), pltpu.SemaphoreType.DMA((copies,))],
        compiler_params=pltpu.CompilerParams(collective_id=0, has_side_effects=True),
        name="gather_bands",
    )(block)


def shards(modes, height, response):
    fields, band_rows, lon_cells = height.shape
    lon_count = lax.axis_size("lon")
    lat_count = lax.axis_size("lat")
    lon_index = lax.axis_index("lon")
    lat_index = lax.axis_index("lat")
    devices = lon_count * lat_count
    cells = lon_count * lon_cells
    device = lon_index * lat_count + lat_index

    order = mode_order(modes, devices)
    local = np.arange(lon_cells)
    angles = (order[:, :, None] * local % cells) * (2.0 * math.pi / cells)
    cos_table = jnp.asarray(np.cos(angles).astype(np.float32))
    sin_table = jnp.asarray(np.sin(angles).astype(np.float32))
    turn = (jnp.asarray(order.astype(np.int32)) * (lon_index * lon_cells) % cells)
    turn = turn.astype(jnp.float32)[:, :, None] * (2.0 * math.pi / cells)
    cos_turn, sin_turn = jnp.cos(turn), jnp.sin(turn)
    table = jnp.stack(
        [
            cos_turn * cos_table - sin_turn * sin_table,
            -(sin_turn * cos_table + cos_turn * sin_table),
        ],
        axis=1,
    ).reshape(2 * modes, lon_cells)

    outputs = []
    for field in range(fields):
        partial = lax.dot_general(
            table, height[field], (((1,), (1,)), ((), ())), precision=high,
            preferred_element_type=jnp.float32,
        )
        spectrum = lax.psum_scatter(partial, "lon", scatter_dimension=0, tiled=True)
        columns = lax.all_to_all(spectrum, "lat", split_axis=0, concat_axis=1, tiled=True)
        synthesis = sweep(columns, response, device, devices, modes, cells)
        bands = lax.all_to_all(synthesis, "lat", split_axis=1, concat_axis=0, tiled=True)
        gathered = gather(bands, lon_count)
        outputs.append(lax.dot_general(
            gathered, table, (((0,), (0,)), ((), ())), precision=high,
            preferred_element_type=jnp.float32,
        ))
    return jnp.stack(outputs)


def solution(mesh):
    placed = (P(None, "lat", "lon"), P())

    def loading(height, response):
        body = functools.partial(shards, response.shape[0])
        return jax.shard_map(
            body, mesh=mesh, in_specs=placed, out_specs=P(None, "lat", "lon"), check_vma=False
        )(height, response)

    return loading
```
